32 devices in a mesh: parts: 2 (over y), tensor: 16 (over z, x, core).
Axes of the slice: x: 2, y: 2, z: 4, core: 2. Of those that a mesh axis runs over, the one named last changes fastest.
Arguments:
- cotangent: bfloat16 [384, 8192], P(('parts', 'tensor')), parts along dimension 0, may hold values from -6 to 6
- hidden: bfloat16 [384, 28672], P('parts', 'tensor'), parts along dimension 0, may hold values from -6 to 6
- down_weight: bfloat16 [28672, 8192], P('tensor'), may hold values from -0.0625 to 0.0625
- adapter_in: bfloat16 [28672, 2560], P('tensor'), may hold values from -0.119628906 to 0.119628906
- adapter_out: bfloat16 [2560, 8192], P(None, 'tensor'), may hold values from -0.0625 to 0.0625
- segment_ids: int32 [384], P('parts'), parts along dimension 0, may hold values from 0 to 11, never falling along the last dimension, each value on 1 to 32 neighbouring positions
- segment_dirs: int32 [24], P('parts'), parts along dimension 0, may hold values from 0 to 39
Outputs:
- grad_hidden: bfloat16 [384, 28672], P('parts', 'tensor'), parts along dimension 0
- grad_in: float32 [57344, 2560], P(('parts', 'tensor')), parts along dimension 0
- grad_out: float32 [5120, 8192], P('parts', 'tensor'), parts along dimension 0
The draws below stay inside these ranges and needn't reach their ends.
There are 2 independent parts, one for each index of `parts`. The reference program is written for one: setup_inputs(seed, part) draws one part's arguments, and reference() takes and returns one part's arrays. A program takes and returns all parts, laid end to end along the dimension named above; an argument that names none is the same for every part. Nothing has to cross between parts.
Inputs may be any that keep to these rules, and one draw needn't show every extreme that they name: `segment_ids`: segment numbers never fall along the tokens; each segment holds 1 to 32 tokens.
All inputs are finite; a program needn't handle non-finite values.
Results may differ from the reference program's by a relative error of at most 0.005.
Values may be sent and summed in bfloat16 or wider, within the bound.
A program may use at most 192 MiB of HBM per device.

```python
import math
import jax
import jax.numpy as jnp
import numpy as np
from jax import lax

D = 8192
FF = 28672
RANK = 64
NUM_DIR = 40
MOST = 32
TOKENS = 192
NSEG = 12


def with_ends(entries, stream_key, least, high):
    longest = entries.shape.index(max(entries.shape))
    spots = []
    for shift in (0, 1):
        where = [jax.random.randint(jax.random.fold_in(stream_key, axis), (), 0, length) for axis, length in enumerate(entries.shape)]
        where[longest] = (where[longest] + shift) % entries.shape[longest]
        spots.append(tuple(where))
    return entries.at[spots[0]].set(least).at[spots[1]].set(high)


def block_levels(own_key, dims, pieces, least, high):
    def one(axis_at, blocks):
        steps = jax.random.uniform(jax.random.fold_in(jax.random.fold_in(own_key, 6), axis_at), (blocks,), jnp.float32, least / len(pieces), high / len(pieces))
        return jnp.repeat(jnp.exp(steps), dims[axis_at] // blocks).reshape((-1,) + (1,) * (len(dims) - axis_at - 1))

    factor_of = one(*pieces[0])
    for cut in pieces[1:]:
        factor_of = factor_of * one(*cut)
    return factor_of


def cumulative_ranks(number_of, slope):
    portions = [(1 << 20) // math.isqrt(rank ** slope) + 1 for rank in range(1, number_of + 1)]
    width = 1 + sum(portions) // (1 << 30)
    return np.cumsum(np.array([max(1, weight // width) for weight in portions]))


def skewed_ids(rng, shape, number_of, lean):
    grid = cumulative_ranks(number_of, lean)
    lot = jax.random.randint(jax.random.fold_in(rng, 1), shape, 0, int(grid[number_of - 1]))
    standing = jnp.searchsorted(jnp.asarray(grid, jnp.int32), lot, side="right")
    return jax.random.permutation(jax.random.fold_in(rng, 2), number_of)[standing].astype(jnp.int32)


def length_profile(number_of, total, limit, skew):
    portions = [(1 << 20) // math.isqrt(rank ** skew) + 1 for rank in range(2, number_of + 1)]
    surplus, counts = total - limit - (number_of - 1), [1] * (number_of - 1)
    while surplus > 0:
        candidates = [i for i in range(number_of - 1) if counts[i] < limit]
        pool, left = sum([portions[i] for i in candidates]), surplus
        for i in candidates:
            more = min(limit - counts[i], max(1, left * portions[i] // pool), surplus)
            counts[i] = counts[i] + more
            surplus = surplus - more
    return np.array([limit] + counts)


def uneven_parts(rng, amount, total, bound, slope):
    if amount == 2:
        one = jax.random.randint(rng, (), max(1, total - bound), min(bound, total - 1) + 1)
        return jnp.stack([one, total - one])
    sizes = jnp.asarray(length_profile(amount, total, bound, slope), jnp.int32)
    pairs = (amount - 1) // 2
    source_of, receiver = sizes[1:1 + 2 * pairs:2], sizes[2:2 + 2 * pairs:2]
    slack = jnp.minimum(source_of - 1, bound - receiver)
    shifted = jax.random.randint(jax.random.fold_in(rng, 1), (pairs,), 0, 1 << 20) % (slack + 1)
    sizes = sizes.at[1:1 + 2 * pairs:2].set(source_of - shifted).at[2:2 + 2 * pairs:2].set(receiver + shifted)
    return sizes[jax.random.permutation(jax.random.fold_in(rng, 2), amount)]


def gaussian(stream_key, shape, scale, most, shards=(), kind=jnp.bfloat16):
    entries = jax.random.normal(stream_key, shape, jnp.float32) * scale
    if len(shards) > 0:
        entries = block_levels(stream_key, shape, shards, -0.22, 0.18) * entries
    return jnp.clip(entries, min=-most, max=most).astype(kind)


def setup_inputs(seed: int = 0, part: int = 0) -> dict:
    key_of = jax.random.split(jax.random.key(seed), 8)
    part_keys = jax.random.split(jax.random.fold_in(key_of[7], part), 8)
    cotangent = gaussian(part_keys[0], (TOKENS, D), 1.0, 6.0, ((0, 16),))
    hidden = gaussian(part_keys[1], (TOKENS, FF), 1.0, 6.0, ((1, 16),))
    down_weight = gaussian(key_of[2], (FF, D), D ** -0.5, 0.0625, ((0, 16),))
    adapter_in = gaussian(key_of[3], (FF, NUM_DIR * RANK), 0.02, 0.119628906, ((0, 16),))
    adapter_out = gaussian(key_of[4], (NUM_DIR * RANK, D), D ** -0.5, 0.0625, ((1, 16),))
    segment_ids = jnp.searchsorted(jnp.cumsum(uneven_parts(part_keys[5], NSEG, TOKENS, MOST, 2)), jnp.arange(TOKENS), side="right").astype(jnp.int32)
    segment_dirs = with_ends(skewed_ids(part_keys[6], (NSEG,), NUM_DIR, 2), jax.random.fold_in(part_keys[6], 3), 0, NUM_DIR - 1).astype(jnp.int32)
    return {"cotangent": cotangent, "hidden": hidden, "down_weight": down_weight, "adapter_in": adapter_in, "adapter_out": adapter_out, "segment_ids": segment_ids, "segment_dirs": segment_dirs}


def reference(cotangent, hidden, down_weight, adapter_in, adapter_out, segment_ids, segment_dirs):
    seg_hot = (segment_ids[:, None] == jnp.arange(NSEG, dtype=jnp.int32)[None, :]).astype(jnp.float32)
    dir_hot = (segment_dirs[:, None] == jnp.arange(NUM_DIR, dtype=jnp.int32)[None, :]).astype(jnp.float32)
    onehot = jnp.dot(seg_hot, dir_hot, precision=lax.Precision.HIGHEST)
    wide_u = lax.dot_general(cotangent, adapter_out, (((1,), (1,)), ((), ())), preferred_element_type=jnp.float32)
    wide_v = jnp.dot(hidden, adapter_in, preferred_element_type=jnp.float32)
    low_u = jnp.sum(wide_u.reshape(TOKENS, NUM_DIR, RANK) * onehot[:, :, None], axis=1)
    low_v = jnp.sum(wide_v.reshape(TOKENS, NUM_DIR, RANK) * onehot[:, :, None], axis=1)
    spread_u = (0.5 * onehot[:, :, None] * low_u[:, None, :]).reshape(TOKENS, NUM_DIR * RANK).astype(jnp.bfloat16)
    spread_v = (0.5 * onehot[:, :, None] * low_v[:, None, :]).reshape(TOKENS, NUM_DIR * RANK).astype(jnp.bfloat16)
    base = lax.dot_general(cotangent, down_weight, (((1,), (1,)), ((), ())), preferred_element_type=jnp.float32)
    extra = lax.dot_general(spread_u, adapter_in, (((1,), (1,)), ((), ())), preferred_element_type=jnp.float32)
    grad_hidden = (base + extra).astype(jnp.bfloat16)
    grad_in = lax.dot_general(hidden, spread_u, (((0,), (0,)), ((), ())), preferred_element_type=jnp.float32)
    grad_out = lax.dot_general(spread_v, cotangent, (((0,), (0,)), ((), ())), preferred_element_type=jnp.float32)
    return (grad_hidden, grad_in, grad_out)
```

```python
import jax
import jax.numpy as jnp
from jax import lax
from jax.sharding import PartitionSpec as P

RANK = 64
NUM_DIR = 40


def direction_table(segment_ids, segment_dirs):
    seg_hot = (
        segment_ids[:, None] == jnp.arange(segment_dirs.shape[0], dtype=jnp.int32)[None, :]
    ).astype(jnp.float32)
    dir_hot = (segment_dirs[:, None] == jnp.arange(NUM_DIR, dtype=jnp.int32)[None, :]).astype(
        jnp.float32
    )
    return jnp.dot(seg_hot, dir_hot, precision=lax.Precision.HIGHEST)


def select_rank(wide, onehot):
    count = wide.shape[0]
    return jnp.sum(wide.reshape(count, NUM_DIR, RANK) * onehot[:, :, None], axis=1)


def spread_rank(low, onehot):
    count = low.shape[0]
    return (
        (0.5 * onehot[:, :, None] * low[:, None, :])
        .reshape(count, NUM_DIR * RANK)
        .astype(jnp.bfloat16)
    )


def gather_blocks(own, shards):
    tiled = jnp.broadcast_to(own[None], (shards,) + own.shape)
    got = lax.all_to_all(tiled, "tensor", 0, 0, tiled=True)
    return got.reshape((shards * own.shape[0],) + own.shape[1:])


def sum_blocks(partial, shards):
    rows = partial.shape[0] // shards
    pieces = partial.reshape((shards, rows) + partial.shape[1:])
    got = lax.all_to_all(pieces, "tensor", 0, 0, tiled=True)
    return gather_blocks(jnp.sum(got, axis=0), shards)


def per_device(cotangent, hidden, down_weight, adapter_in, adapter_out, segment_ids, segment_dirs):
    onehot = direction_table(segment_ids, segment_dirs)
    width_share = adapter_out.shape[1]
    shards = cotangent.shape[1] // width_share
    own = cotangent.shape[0]
    full_rows = lax.all_gather(cotangent, "tensor", axis=0, tiled=True)
    pieces = cotangent.reshape(own, shards, width_share).transpose(1, 0, 2)
    columns = lax.all_to_all(pieces, "tensor", 0, 0, tiled=True).reshape(
        shards * own, width_share
    )
    wide_u = lax.dot_general(
        columns, adapter_out, (((1,), (1,)), ((), ())), preferred_element_type=jnp.float32
    )
    wide_v = jnp.dot(hidden, adapter_in, preferred_element_type=jnp.float32)
    part = jnp.concatenate([select_rank(wide_u, onehot), select_rank(wide_v, onehot)], axis=1)
    low = sum_blocks(part, shards)
    spread_u = spread_rank(low[:, :RANK], onehot)
    spread_v = spread_rank(low[:, RANK:], onehot)
    grad_in = lax.dot_general(
        hidden, spread_u, (((0,), (0,)), ((), ())), preferred_element_type=jnp.float32
    )
    grad_out = lax.dot_general(
        spread_v, columns, (((0,), (0,)), ((), ())), preferred_element_type=jnp.float32
    )
    extra = lax.dot_general(
        spread_u, adapter_in, (((1,), (1,)), ((), ())), preferred_element_type=jnp.float32
    )
    base = lax.dot_general(
        full_rows, down_weight, (((1,), (1,)), ((), ())), preferred_element_type=jnp.float32
    )
    grad_hidden = (base + extra).astype(jnp.bfloat16)
    return (grad_hidden, grad_in, grad_out)


def solution(mesh):
    return jax.shard_map(
        per_device,
        mesh=mesh,
        in_specs=(
            P(("parts", "tensor"), None),
            P("parts", "tensor"),
            P("tensor", None),
            P("tensor", None),
            P(None, "tensor"),
            P("parts"),
            P("parts"),
        ),
        out_specs=(P("parts", "tensor"), P(("parts", "tensor"), None), P("parts", "tensor")),
        check_vma=False,
    )
```

```python
import jax
import jax.numpy as jnp
from jax import lax
from jax.experimental import pallas as pl
from jax.sharding import PartitionSpec as P

RANK = 64
NUM_DIR = 40


def direction_table(segment_ids, segment_dirs):
    seg_hot = (
        segment_ids[:, None] == jnp.arange(segment_dirs.shape[0], dtype=jnp.int32)[None, :]
    ).astype(jnp.float32)
    dir_hot = (segment_dirs[:, None] == jnp.arange(NUM_DIR, dtype=jnp.int32)[None, :]).astype(
        jnp.float32
    )
    return jnp.dot(seg_hot, dir_hot, precision=lax.Precision.HIGHEST)


def select_rank(wide, onehot):
    count = wide.shape[0]
    return jnp.sum(wide.reshape(count, NUM_DIR, RANK) * onehot[:, :, None], axis=1)


def spread_rank(low, onehot):
    count = low.shape[0]
    return (
        (0.5 * onehot[:, :, None] * low[:, None, :])
        .reshape(count, NUM_DIR * RANK)
        .astype(jnp.bfloat16)
    )


def _rows_kernel(lhs_ref, rhs_ref, out_ref):
    out_ref[...] = jnp.dot(lhs_ref[...], rhs_ref[...], preferred_element_type=jnp.float32)


def rows_matmul(lhs, rhs):
    m, k = lhs.shape
    n = rhs.shape[1]
    tile = next((t for t in (512, 256, 128) if m % t == 0), m)
    return pl.pallas_call(
        _rows_kernel,
        grid=(m // tile,),
        in_specs=[
            pl.BlockSpec((tile, k), lambda i: (i, 0)),
            pl.BlockSpec((k, n), lambda i: (0, 0)),
        ],
        out_specs=pl.BlockSpec((tile, n), lambda i: (i, 0)),
        out_shape=jax.ShapeDtypeStruct((m, n), jnp.float32),
    )(lhs, rhs)


def gather_blocks(own, shards):
    tiled = jnp.broadcast_to(own[None], (shards,) + own.shape)
    got = lax.all_to_all(tiled, "tensor", 0, 0, tiled=True)
    return got.reshape((shards * own.shape[0],) + own.shape[1:])


def sum_blocks(partial, shards):
    rows = partial.shape[0] // shards
    pieces = partial.reshape((shards, rows) + partial.shape[1:])
    got = lax.all_to_all(pieces, "tensor", 0, 0, tiled=True)
    return gather_blocks(jnp.sum(got, axis=0), shards)


def per_device(cotangent, hidden, down_weight, adapter_in, adapter_out, segment_ids, segment_dirs):
    onehot = direction_table(segment_ids, segment_dirs)
    width_share = adapter_out.shape[1]
    shards = cotangent.shape[1] // width_share
    own = cotangent.shape[0]
    full_rows = lax.all_gather(cotangent, "tensor", axis=0, tiled=True)
    pieces = cotangent.reshape(own, shards, width_share).transpose(1, 0, 2)
    columns = lax.all_to_all(pieces, "tensor", 0, 0, tiled=True).reshape(
        shards * own, width_share
    )
    wide_u = lax.dot_general(
        columns, adapter_out, (((1,), (1,)), ((), ())), preferred_element_type=jnp.float32
    )
    wide_v = jnp.dot(hidden, adapter_in, preferred_element_type=jnp.float32)
    part = jnp.concatenate([select_rank(wide_u, onehot), select_rank(wide_v, onehot)], axis=1)
    low = sum_blocks(part, shards)
    spread_u = spread_rank(low[:, :RANK], onehot)
    spread_v = spread_rank(low[:, RANK:], onehot)
    grad_in = rows_matmul(hidden.T, spread_u)
    grad_out = lax.dot_general(
        spread_v, columns, (((0,), (0,)), ((), ())), preferred_element_type=jnp.float32
    )
    extra = lax.dot_general(
        spread_u, adapter_in, (((1,), (1,)), ((), ())), preferred_element_type=jnp.float32
    )
    base = lax.dot_general(
        full_rows, down_weight, (((1,), (1,)), ((), ())), preferred_element_type=jnp.float32
    )
    grad_hidden = (base + extra).astype(jnp.bfloat16)
    return (grad_hidden, grad_in, grad_out)


def solution(mesh):
    return jax.shard_map(
        per_device,
        mesh=mesh,
        in_specs=(
            P(("parts", "tensor"), None),
            P("parts", "tensor"),
            P("tensor", None),
            P("tensor", None),
            P(None, "tensor"),
            P("parts"),
            P("parts"),
        ),
        out_specs=(P("parts", "tensor"), P(("parts", "tensor"), None), P("parts", "tensor")),
        check_vma=False,
    )
```

```python
import jax
import jax.numpy as jnp
from jax import lax
from jax.experimental import pallas as pl
from jax.sharding import PartitionSpec as P

RANK = 64
NUM_DIR = 40


def direction_table(segment_ids, segment_dirs):
    seg_hot = (
        segment_ids[:, None] == jnp.arange(segment_dirs.shape[0], dtype=jnp.int32)[None, :]
    ).astype(jnp.float32)
    dir_hot = (segment_dirs[:, None] == jnp.arange(NUM_DIR, dtype=jnp.int32)[None, :]).astype(
        jnp.float32
    )
    return jnp.dot(seg_hot, dir_hot, precision=lax.Precision.HIGHEST)


def select_rank(wide, onehot):
    count = wide.shape[0]
    return jnp.sum(wide.reshape(count, NUM_DIR, RANK) * onehot[:, :, None], axis=1)


def spread_rank(low, onehot):
    count = low.shape[0]
    return (
        (0.5 * onehot[:, :, None] * low[:, None, :])
        .reshape(count, NUM_DIR * RANK)
        .astype(jnp.bfloat16)
    )


def _rows_kernel(lhs_ref, rhs_ref, out_ref):
    out_ref[...] = jnp.dot(lhs_ref[...], rhs_ref[...], preferred_element_type=jnp.float32)


def rows_matmul(lhs, rhs):
    m, k = lhs.shape
    n = rhs.shape[1]
    tile = next((t for t in (512, 256, 128) if m % t == 0), m)
    return pl.pallas_call(
        _rows_kernel,
        grid=(m // tile,),
        in_specs=[
            pl.BlockSpec((tile, k), lambda i: (i, 0)),
            pl.BlockSpec((k, n), lambda i: (0, 0)),
        ],
        out_specs=pl.BlockSpec((tile, n), lambda i: (i, 0)),
        out_shape=jax.ShapeDtypeStruct((m, n), jnp.float32),
    )(lhs, rhs)


def gather_blocks(own, shards):
    tiled = jnp.broadcast_to(own[None], (shards,) + own.shape)
    got = lax.all_to_all(tiled, "tensor", 0, 0, tiled=True)
    return got.reshape((shards * own.shape[0],) + own.shape[1:])


def sum_blocks(partial, shards):
    if shards <= 16:
        tiled = jnp.broadcast_to(partial[None], (shards,) + partial.shape)
        return jnp.sum(lax.all_to_all(tiled, "tensor", 0, 0, tiled=True), axis=0)
    rows = partial.shape[0] // shards
    pieces = partial.reshape((shards, rows) + partial.shape[1:])
    got = lax.all_to_all(pieces, "tensor", 0, 0, tiled=True)
    return gather_blocks(jnp.sum(got, axis=0), shards)


def per_device(cotangent, hidden, down_weight, adapter_in, adapter_out, segment_ids, segment_dirs):
    onehot = direction_table(segment_ids, segment_dirs)
    width_share = adapter_out.shape[1]
    shards = cotangent.shape[1] // width_share
    own = cotangent.shape[0]
    full_rows = lax.all_gather(cotangent, "tensor", axis=0, tiled=True)
    pieces = cotangent.reshape(own, shards, width_share).transpose(1, 0, 2)
    columns = lax.all_to_all(pieces, "tensor", 0, 0, tiled=True).reshape(
        shards * own, width_share
    )
    wide_u = lax.dot_general(
        columns, adapter_out, (((1,), (1,)), ((), ())), preferred_element_type=jnp.float32
    )
    wide_v = jnp.dot(hidden, adapter_in, preferred_element_type=jnp.float32)
    part = jnp.concatenate([select_rank(wide_u, onehot), select_rank(wide_v, onehot)], axis=1)
    low = sum_blocks(part, shards)
    spread_u = spread_rank(low[:, :RANK], onehot)
    spread_v = spread_rank(low[:, RANK:], onehot)
    grad_in = rows_matmul(hidden.T, spread_u)
    grad_out = lax.dot_general(
        spread_v, columns, (((0,), (0,)), ((), ())), preferred_element_type=jnp.float32
    )
    extra = lax.optimization_barrier(
        lax.dot_general(
            spread_u, adapter_in, (((1,), (1,)), ((), ())), preferred_element_type=jnp.float32
        )
    )
    base = lax.dot_general(
        full_rows, down_weight, (((1,), (1,)), ((), ())), preferred_element_type=jnp.float32
    )
    grad_hidden = (base + extra).astype(jnp.bfloat16)
    return (grad_hidden, grad_in, grad_out)


def solution(mesh):
    return jax.shard_map(
        per_device,
        mesh=mesh,
        in_specs=(
            P(("parts", "tensor"), None),
            P("parts", "tensor"),
            P("tensor", None),
            P("tensor", None),
            P(None, "tensor"),
            P("parts"),
            P("parts"),
        ),
        out_specs=(P("parts", "tensor"), P(("parts", "tensor"), None), P("parts", "tensor")),
        check_vma=False,
    )
```

```python
import jax
import jax.numpy as jnp
from jax import lax
from jax.experimental import pallas as pl
from jax.sharding import PartitionSpec as P

RANK = 64
NUM_DIR = 40


def direction_table(segment_ids, segment_dirs):
    seg_hot = (
        segment_ids[:, None] == jnp.arange(segment_dirs.shape[0], dtype=jnp.int32)[None, :]
    ).astype(jnp.float32)
    dir_hot = (segment_dirs[:, None] == jnp.arange(NUM_DIR, dtype=jnp.int32)[None, :]).astype(
        jnp.float32
    )
    return jnp.dot(seg_hot, dir_hot, precision=lax.Precision.HIGHEST)


def select_rank(wide, onehot):
    count = wide.shape[0]
    return jnp.sum(wide.reshape(count, NUM_DIR, RANK) * onehot[:, :, None], axis=1)


def spread_rank(low, onehot):
    count = low.shape[0]
    return (
        (0.5 * onehot[:, :, None] * low[:, None, :])
        .reshape(count, NUM_DIR * RANK)
        .astype(jnp.bfloat16)
    )


def _rows_kernel(lhs_ref, rhs_ref, out_ref):
    out_ref[...] = jnp.dot(lhs_ref[...], rhs_ref[...], preferred_element_type=jnp.float32)


def rows_matmul(lhs, rhs):
    m, k = lhs.shape
    n = rhs.shape[1]
    tile = next((t for t in (512, 256, 128) if m % t == 0), m)
    return pl.pallas_call(
        _rows_kernel,
        grid=(m // tile,),
        in_specs=[
            pl.BlockSpec((tile, k), lambda i: (i, 0)),
            pl.BlockSpec((k, n), lambda i: (0, 0)),
        ],
        out_specs=pl.BlockSpec((tile, n), lambda i: (i, 0)),
        out_shape=jax.ShapeDtypeStruct((m, n), jnp.float32),
    )(lhs, rhs)


def gather_blocks(own, shards):
    tiled = jnp.broadcast_to(own[None], (shards,) + own.shape)
    got = lax.all_to_all(tiled, "tensor", 0, 0, tiled=True)
    return got.reshape((shards * own.shape[0],) + own.shape[1:])


def sum_blocks(partial, shards):
    rows = partial.shape[0] // shards
    pieces = partial.reshape((shards, rows) + partial.shape[1:])
    got = lax.all_to_all(pieces, "tensor", 0, 0, tiled=True)
    return gather_blocks(jnp.sum(got, axis=0), shards)


def per_device(cotangent, hidden, down_weight, adapter_in, adapter_out, segment_ids, segment_dirs):
    onehot = direction_table(segment_ids, segment_dirs)
    width_share = adapter_out.shape[1]
    shards = cotangent.shape[1] // width_share
    own = cotangent.shape[0]
    full_rows = lax.all_gather(cotangent, "tensor", axis=0, tiled=True)
    pieces = cotangent.reshape(own, shards, width_share).transpose(1, 0, 2)
    columns = lax.all_to_all(pieces, "tensor", 0, 0, tiled=True).reshape(
        shards * own, width_share
    )
    wide_u = lax.dot_general(
        columns, adapter_out, (((1,), (1,)), ((), ())), preferred_element_type=jnp.float32
    )
    wide_v = jnp.dot(hidden, adapter_in, preferred_element_type=jnp.float32)
    part = jnp.concatenate([select_rank(wide_u, onehot), select_rank(wide_v, onehot)], axis=1)
    low = sum_blocks(part, shards)
    spread_u = spread_rank(low[:, :RANK], onehot)
    spread_v = spread_rank(low[:, RANK:], onehot)
    grad_in = rows_matmul(hidden.T, spread_u)
    grad_out = lax.dot_general(
        spread_v, columns, (((0,), (0,)), ((), ())), preferred_element_type=jnp.float32
    )
    extra = lax.optimization_barrier(
        lax.dot_general(
            spread_u, adapter_in, (((1,), (1,)), ((), ())), preferred_element_type=jnp.float32
        )
    )
    base = lax.dot_general(
        full_rows, down_weight, (((1,), (1,)), ((), ())), preferred_element_type=jnp.float32
    )
    grad_hidden = (base + extra).astype(jnp.bfloat16)
    return (grad_hidden, grad_in, grad_out)


def solution(mesh):
    return jax.shard_map(
        per_device,
        mesh=mesh,
        in_specs=(
            P(("parts", "tensor"), None),
            P("parts", "tensor"),
            P("tensor", None),
            P("tensor", None),
            P(None, "tensor"),
            P("parts"),
            P("parts"),
        ),
        out_specs=(P("parts", "tensor"), P(("parts", "tensor"), None), P("parts", "tensor")),
        check_vma=False,
    )
```
